32 devices in a mesh: gauge: 8 (over y, x, core), focus: 4 (over z).
Axes of the slice: x: 2, y: 2, z: 4, core: 2. Of those that a mesh axis runs over, the one named last changes fastest.
Arguments:
- aerial_clips: bfloat16 [4, 512, 8192], P('focus', 'gauge'), may hold values from 0 to 1
- basis_terms: bfloat16 [8192, 512], replicated, may hold values from -0.0625 to 0.0625
- holder: int32 [4, 512, 2], P('focus', 'gauge'), may hold values from 0 to 7, all different within a row; in each aligned block of 64 rows (0 to 63, 64 to 127, ..., all dimensions but the last counted through in order) at most 32 rows name the same one
- cache_slot: int32 [4, 512, 2], P('focus', 'gauge'), may hold values from 0 to 63
- dose_index: int32 [4, 512, 11], P('focus', 'gauge'), may hold values from 0 to 15
- dose_levels: float32 [16], replicated, may hold values from 0.7 to 1.4
- threshold: float32 [4], P('focus'), may hold values from 0.3 to 0.7
- measured: float32 [4, 512, 11], P('focus', 'gauge'), may hold values from -3 to 3
- parameters: float32 [512], replicated, may hold values from -0.25 to 0.25
Outputs:
- upper_factor: float32 [512, 512], replicated
- new_params: float32 [512], replicated
- linear_residual: float32 [4, 512, 11], P('focus', 'gauge')
The draws below stay inside these ranges and needn't reach their ends.
Inputs may be any that keep to these rules, and one draw needn't show every extreme that they name: A gauge's two exposures have different holders; among the 64 gauges of one device no holder is named more than 32 times.
All inputs are finite; a program needn't handle non-finite values.
Results may differ from the reference program's by a relative error of at most 0.0013.
Values may be sent and summed in bfloat16 or wider, within the bound.
No kernel may reach another device: no remote copies, remote signals or barrier semaphores. Data moves between devices by JAX's collectives and lax.ppermute only.
A program may use at most 256 MiB of HBM per device.

```python
import math
import jax
import jax.numpy as jnp
import numpy as np
from jax import lax

P_SIZE = 512
PIX = 8192
DOSES = 16
DOSE_ROWS = 11
G_DEV = 64
CL_DEV = 64
CAP = 32
NF = 4
GAUGES = 512
CLIPS = 512
N_GAUGE = 8


def set_ends(result, own_key, least, largest):
    longest = result.shape.index(max(result.shape))
    spots = []
    for shift in (0, 1):
        where = [jax.random.randint(jax.random.fold_in(own_key, axis), (), 0, length) for axis, length in enumerate(result.shape)]
        where[longest] = (where[longest] + shift) % result.shape[longest]
        spots.append(tuple(where))
    return result.at[spots[0]].set(least).at[spots[1]].set(largest)


def level_of(rng, extent, split, smallest, high):
    level = 1.0
    for position, shards_of in split:
        steps = jax.random.uniform(jax.random.fold_in(jax.random.fold_in(rng, 6), position), (shards_of,), jnp.float32, smallest / len(split), high / len(split))
        level = level * jnp.repeat(jnp.exp(steps), extent[position] // shards_of).reshape((-1,) + (1,) * (len(extent) - 1 - position))
    return level


def routed_block(own_key, own, number, rows, count, top, bound, slope):
    order = jax.random.permutation(own_key, count)
    packed, usual = portions_of(count, rows * top, bound, slope, True), portions_of(count, rows * top, bound, slope, False)
    places = jnp.arange(count)

    def named(lengths, turn):
        used = int((lengths > 0).sum())
        fixed = max(1, used // 4)
        passed = fixed + (places - fixed + turn * (used - fixed)) % max(1, count - fixed)
        return jnp.zeros((count,), jnp.int32).at[order[jnp.where(places < fixed, places, passed)]].set(jnp.asarray(lengths, jnp.int32))

    lengths = jnp.where(number % 4 == 0, named(packed, number // 4), named(usual, number - number // 4 - 1))
    mixed = jax.random.permutation(jax.random.fold_in(own, 3), count)
    giver, taker = mixed[0:count // 2 * 2:2], mixed[1:count // 2 * 2:2]
    room = jnp.minimum(lengths[giver] - 1, bound - lengths[taker]) // 2
    room = jnp.where((giver == order[0]) | (taker == order[0]) | (lengths[taker] == 0), 0, jnp.maximum(room, 0))
    passed = jax.random.randint(jax.random.fold_in(own, 4), (count // 2,), 0, 1 << 20) % (room + 1)
    lengths = lengths.at[giver].add(-passed).at[taker].add(passed)
    items = jnp.searchsorted(jnp.cumsum(lengths), jnp.arange(rows * top), side="right").astype(jnp.int32)
    table = items.reshape(top, rows).T
    table = table[jax.random.permutation(jax.random.fold_in(own, 1), rows)]
    turn = jax.random.randint(jax.random.fold_in(own, 2), (rows, 1), 0, top)
    return jnp.take_along_axis(table, (jnp.arange(top)[None, :] + turn) % top, axis=1)


def portions_of(number_of, total, limit, lean, full):
    portions = [(1 << 20) // math.isqrt(standing ** lean) + 1 for standing in range(1, number_of + 1)]
    largest = limit if full else min(limit, max(-(-total // number_of), total * portions[0] // sum(portions)))
    least = 1 if total - largest >= number_of - 1 else 0
    given, rest = [largest] + [least] * (number_of - 1), total - largest - least * (number_of - 1)
    while rest > 0:
        movable = [i for i in range(1, number_of) if given[i] < largest] or [i for i in range(1, number_of) if given[i] < limit]
        whole, left = sum([portions[i] for i in movable]), rest
        for i in movable:
            addition = min(limit - given[i], max(1, left * portions[i] // whole), rest)
            given[i] = given[i] + addition
            rest = rest - addition
    return np.array(given)


def scatter_about(stream_key, extent, width, most, split=(), kind=jnp.bfloat16):
    entries = jax.random.normal(stream_key, extent, jnp.float32) * width
    if len(split) > 0:
        entries = level_of(stream_key, extent, split, -0.22, 0.18) * entries
    return jnp.clip(entries, min=-most, max=most).astype(kind)


def setup_inputs(seed: int = 0) -> dict:
    seeds = jax.random.split(jax.random.key(seed), 10)
    aerial_clips = jnp.clip(1.0 * jax.random.uniform(seeds[0], (NF, CLIPS, PIX), jnp.float32) ** level_of(seeds[0], (NF, CLIPS, PIX), ((0, 4), (1, 8)), -0.2, 0.2), 0.0, 1.0).astype(jnp.bfloat16)
    basis_terms = scatter_about(seeds[1], (PIX, P_SIZE), PIX ** -0.5, 0.0625)
    holder_keys = jax.random.split(jax.random.fold_in(seeds[2], 1), NF * GAUGES // G_DEV)
    holder_turns = jax.random.permutation(jax.random.fold_in(seeds[2], 3), NF * GAUGES // G_DEV)
    holder = jax.vmap(lambda own, number: routed_block(jax.random.fold_in(seeds[2], 2), own, number, G_DEV, N_GAUGE, 2, CAP, 2))(holder_keys, holder_turns).reshape((NF, GAUGES, 2))
    cache_slot = set_ends(jax.random.randint(seeds[3], (NF, GAUGES, 2), 0, CL_DEV), jax.random.fold_in(seeds[3], 1), 0, CL_DEV - 1).astype(jnp.int32)
    dose_index = set_ends(jax.random.randint(seeds[4], (NF, GAUGES, DOSE_ROWS), 0, DOSES), jax.random.fold_in(seeds[4], 1), 0, DOSES - 1).astype(jnp.int32)
    dose_levels = jnp.clip(jnp.exp(jax.random.uniform(seeds[5], (DOSES,), jnp.float32, math.log(0.7), math.log(1.4))), 0.7, 1.4)
    threshold = jnp.clip(0.3 + 0.39999998 * jax.random.uniform(seeds[6], (NF,), jnp.float32) ** level_of(seeds[6], (NF,), ((0, 4),), -0.2, 0.2), 0.3, 0.7)
    measured = scatter_about(seeds[7], (NF, GAUGES, DOSE_ROWS), 0.5, 3.0, ((0, 4), (1, 8)), jnp.float32)
    parameters = scatter_about(seeds[8], (P_SIZE,), P_SIZE ** -0.5, 0.25, (), jnp.float32)
    return dict(aerial_clips=aerial_clips, basis_terms=basis_terms, holder=holder, cache_slot=cache_slot, dose_index=dose_index, dose_levels=dose_levels, threshold=threshold, measured=measured, parameters=parameters)


DAMPING = 0.05
STEEPNESS = 4.0

def gauge_rows(inputs, basis_terms, dose_levels, parameters):
    clip_block, holder_block, slot_block, index_block, level, measured_block = inputs
    clip_ids = (holder_block.astype(jnp.int32) * CL_DEV + slot_block.astype(jnp.int32)).reshape(-1)
    clip_pairs = jnp.take(clip_block, clip_ids, axis=0).astype(jnp.float32).reshape(GAUGES, 2, PIX)
    intensity = 0.5 * (clip_pairs[:, 0] + clip_pairs[:, 1])
    dose_rows = dose_levels[index_block.astype(jnp.int32)]
    response = jnp.tanh(STEEPNESS * (dose_rows[:, :, None] * intensity[:, None, :] - level)).astype(jnp.bfloat16)
    features = jnp.dot(response.reshape(GAUGES * DOSE_ROWS, PIX).astype(jnp.float32), basis_terms.astype(jnp.float32), preferred_element_type=jnp.float32)
    linear = jnp.dot(features, parameters, precision=lax.Precision.HIGHEST)
    signal = jnp.tanh(linear)
    derivative = 1.0 - signal * signal
    misfit = measured_block.reshape(-1) - signal
    scale = float(NF * GAUGES * DOSE_ROWS) ** (-0.5)
    jacobian = scale * derivative[:, None] * features
    normal_mat = jnp.dot(jacobian.T, jacobian, precision=lax.Precision.HIGHEST)
    projected = jnp.dot(jacobian.T, scale * misfit, precision=lax.Precision.HIGHEST)
    return (normal_mat, projected, features, misfit, derivative)

def reference(aerial_clips, basis_terms, holder, cache_slot, dose_index, dose_levels, threshold, measured, parameters):

    def one_focus(inputs):
        return gauge_rows(inputs, basis_terms, dose_levels, parameters)
    normal_mat, projected, features, misfit, derivative = lax.map(one_focus, (aerial_clips, holder, cache_slot, dose_index, threshold, measured))
    identity = jnp.eye(P_SIZE, dtype=jnp.float32)
    combined = jnp.sum(normal_mat, axis=0) + DAMPING * identity
    summed = jnp.sum(projected, axis=0)
    lower_factor = jnp.linalg.cholesky(combined)
    carried = jax.scipy.linalg.solve_triangular(lower_factor, summed, lower=True)
    update = jax.scipy.linalg.solve_triangular(lower_factor.T, carried, lower=False)
    new_params = parameters + update
    moved = jnp.einsum('frp,p->fr', features, update, precision=lax.Precision.HIGHEST)
    linear_residual = (misfit - derivative * moved).reshape(NF, GAUGES, DOSE_ROWS)
    return (lower_factor.T, new_params, linear_residual)
```

```python
import functools

import jax
import jax.numpy as jnp
from jax import lax
from jax.experimental import pallas as pl
from jax.experimental.pallas import tpu as pltpu
from jax.sharding import PartitionSpec as P

DAMPING = 0.05
STEEPNESS = 4.0
TILE = 128
GROUP = 8
HALVINGS = 3
PIECES = 1 << HALVINGS
PIECE_ROWS = TILE + 8
CHUNKS = 4
VMEM_BYTES = 56 << 20
HIGHEST = lax.Precision.HIGHEST


def bits_of(size):
    return [1 << k for k in range(size.bit_length() - 1)]


def flipped(place):
    return sum(((place >> k) & 1) << (HALVINGS - 1 - k) for k in range(HALVINGS))


def swap(value, axis, bit):
    size = lax.axis_size(axis)
    return lax.ppermute(value, axis, [(i, i ^ bit) for i in range(size)])


def dot_rows(left, right):
    return lax.dot_general(
        left, right, (((0,), (0,)), ((), ())), precision=HIGHEST, preferred_element_type=jnp.float32
    )


def dot_plain(left, right):
    return lax.dot_general(
        left, right, (((1,), (0,)), ((), ())), precision=HIGHEST, preferred_element_type=jnp.float32
    )


def dot_columns(left, right):
    return lax.dot_general(
        left, right, (((1,), (1,)), ((), ())), precision=HIGHEST, preferred_element_type=jnp.float32
    )


def full(value):
    return jnp.broadcast_to(value, (8, TILE))


def piece_table(count):
    table = []
    for b in range(0, count, 2):
        table.append((b, b + 1, True))
    for r in range(count):
        for c in range(r + 1, count):
            table.append((r, c, False))
    return table


def resist_kernel(first, gauges, doses, block_ref, threshold_ref, dose_ref, select_ref, *refs):
    pieces = refs[: len(refs) - (3 if first else 4)]
    rest = refs[len(pieces) :]
    basis_ref = rest[0]
    out_ref, rows_ref = rest[-2], rest[-1]
    width = pieces[0].shape[0]
    picked = None
    for o, piece in enumerate(pieces):
        term = jnp.dot(
            select_ref[:, o * width : (o + 1) * width],
            piece[...],
            preferred_element_type=jnp.float32,
        )
        picked = term if picked is None else picked + term
    level = threshold_ref[0]
    for d in range(doses):
        answer = jnp.tanh(dose_ref[:, d : d + 1] * picked - level).astype(jnp.bfloat16)
        for who in range(2):
            low = (who * doses + d) * gauges
            rows_ref[low : low + gauges, :] = answer[who * gauges : (who + 1) * gauges, :]
    summed = jnp.dot(rows_ref[...], basis_ref[...], preferred_element_type=jnp.float32)
    if first:
        out_ref[...] = summed
    else:
        out_ref[...] = rest[1][...] + summed


def resist_rows(block, threshold, doses_by_gauge, select, pieces, basis, total, doses):
    pair = pieces[0].shape[0]
    gauges = doses_by_gauge.shape[0] // 2
    pixels = pieces[0].shape[1]
    terms = basis.shape[1]
    rows = 2 * gauges * doses
    first = total is None
    whole = lambda shape: pl.BlockSpec(shape, lambda i, s: (0, 0))
    in_specs = [
        pl.BlockSpec(memory_space=pltpu.SMEM),
        whole(doses_by_gauge.shape),
        whole(select.shape),
        *[whole((pair, pixels)) for _ in pieces],
        pl.BlockSpec((pixels, terms), lambda i, s: (s[0], 0)),
    ]
    operands = [threshold, doses_by_gauge, select, *pieces, basis]
    if not first:
        in_specs.append(whole((rows, terms)))
        operands.append(total)
    return pl.pallas_call(
        functools.partial(resist_kernel, first, gauges, doses),
        out_shape=jax.ShapeDtypeStruct((rows, terms), jnp.float32),
        grid_spec=pltpu.PrefetchScalarGridSpec(
            num_scalar_prefetch=1,
            grid=(1,),
            in_specs=in_specs,
            out_specs=whole((rows, terms)),
            scratch_shapes=[pltpu.VMEM((rows, pixels), jnp.bfloat16)],
        ),
        input_output_aliases={} if first else {len(operands): 0},
        compiler_params=pltpu.CompilerParams(vmem_limit_bytes=VMEM_BYTES),
        cost_estimate=pl.CostEstimate(
            flops=2 * rows * pixels * terms,
            bytes_accessed=2 * pixels * (terms + pair * len(pieces)) + 8 * rows * terms,
            transcendentals=rows * pixels,
        ),
        name="resist",
    )(block, *operands)


def normal_kernel(scale, table, me_ref, mine_ref, other_ref, measured_ref, params_ref, feat_ref, misfit_ref, deriv_ref, out_ref, jac_ref):
    gauges, doses = measured_ref.shape
    terms = mine_ref.shape[1]
    count = terms // TILE
    me = me_ref[0]
    params = params_ref[...]
    lane = lax.broadcasted_iota(jnp.int32, (gauges, doses), 1)
    linear = jnp.zeros((gauges, doses), jnp.float32)
    for d in range(doses):
        low, high = d * gauges, (d + 1) * gauges
        feat = mine_ref[low:high, :] + other_ref[low:high, :]
        feat_ref[low:high, :] = feat
        along = jnp.sum(feat * params, axis=1, keepdims=True)
        linear = jnp.where(lane == d, along, linear)
    signal = jnp.tanh(linear)
    deriv = 1.0 - signal * signal
    misfit = measured_ref[...] - signal
    deriv_ref[...] = deriv
    misfit_ref[...] = misfit
    projected = jnp.zeros((1, terms), jnp.float32)
    for d in range(doses):
        low, high = d * gauges, (d + 1) * gauges
        jac = (scale * deriv[:, d : d + 1]) * feat_ref[low:high, :]
        jac_ref[low:high, :] = jac
        projected = projected + jnp.sum(jac * (scale * misfit[:, d : d + 1]), axis=0, keepdims=True)
    row = lax.broadcasted_iota(jnp.int32, (TILE, TILE), 0)
    col = lax.broadcasted_iota(jnp.int32, (TILE, TILE), 1)
    blocks = {}
    for b in range(count):
        strip = dot_rows(jac_ref[:, b * TILE : (b + 1) * TILE], jac_ref[:, b * TILE :])
        for c in range(b, count):
            blocks[b, c] = strip[:, (c - b) * TILE : (c - b + 1) * TILE]
    extra = [projected[:, b * TILE : (b + 1) * TILE] for b in range(count)]
    for p, (r, c, paired) in enumerate(table):
        where = flipped(p ^ me)
        if paired:
            second = blocks[c, c]
            block = jnp.where(row <= col, blocks[r, r], second)
            extra.append(jnp.sum(jnp.where(row == col, second, 0.0), axis=0, keepdims=True))
        else:
            block = blocks[r, c]
        out_ref[where, :TILE, :] = block
        out_ref[where, TILE:, :] = jnp.zeros((8, TILE), jnp.float32)
    home = flipped(me)
    for k, line in enumerate(extra):
        out_ref[home, TILE + k : TILE + k + 1, :] = line


def factor_tile(block):
    count = TILE // GROUP
    sub = lax.broadcasted_iota(jnp.int32, (8, TILE), 0)
    lane = lax.broadcasted_iota(jnp.int32, (8, TILE), 1)
    left = [block[8 * q : 8 * q + 8, :] for q in range(count)]
    right = [jnp.where(lane == sub + 8 * q, 1.0, 0.0).astype(jnp.float32) for q in range(count)]
    for p in range(count):
        base = GROUP * p
        cols = [full(left[p][:, base + k : base + k + 1]) for k in range(GROUP)]
        a = [[full(cols[k][m : m + 1, :]) if m >= k else None for k in range(GROUP)] for m in range(GROUP)]
        low = [[None] * GROUP for _ in range(GROUP)]
        root = []
        for k in range(GROUP):
            inverse = 1.0 / a[k][k]
            root.append(lax.rsqrt(a[k][k]))
            for m in range(k + 1, GROUP):
                for j in range(k + 1, m + 1):
                    a[m][j] = a[m][j] - (a[m][k] * a[j][k]) * inverse
        for k in range(GROUP):
            for m in range(k + 1, GROUP):
                low[m][k] = a[m][k] * root[k]
        upper = [full(left[p][k : k + 1, :]) for k in range(GROUP)]
        other = [full(right[p][k : k + 1, :]) for k in range(GROUP)]
        for k in range(GROUP):
            upper[k] = upper[k] * root[k]
            other[k] = other[k] * root[k]
            for m in range(k + 1, GROUP):
                upper[m] = upper[m] - low[m][k] * upper[k]
                other[m] = other[m] - low[m][k] * other[k]
        for q in range(p + 1, count):
            c = [full(left[q][:, base + k : base + k + 1]) for k in range(GROUP)]
            for k in range(GROUP):
                c[k] = c[k] * root[k]
                for m in range(k + 1, GROUP):
                    c[m] = c[m] - low[m][k] * c[k]
            for k in range(GROUP):
                left[q] = left[q] - c[k] * upper[k]
                right[q] = right[q] - c[k] * other[k]
        new_left, new_right = upper[GROUP - 1], other[GROUP - 1]
        for k in range(GROUP - 1):
            new_left = jnp.where(sub == k, upper[k], new_left)
            new_right = jnp.where(sub == k, other[k], new_right)
        left[p] = jnp.where(lane >= sub + base, new_left, 0.0)
        right[p] = new_right
    return left, right


def factor_kernel(table, groups, me_ref, *refs):
    sources = refs[: len(groups)]
    feat_ref, misfit_ref, deriv_ref, params_ref, upper_ref, new_ref, resid_ref, stage, work, inv, rhs = refs[len(groups) :]
    terms = work.shape[0]
    count = terms // TILE
    me = me_ref[0]
    for source, places in zip(sources, groups):
        for k, place in enumerate(places):
            stage[place ^ me] = source[k]
    row = lax.broadcasted_iota(jnp.int32, (TILE, TILE), 0)
    col = lax.broadcasted_iota(jnp.int32, (TILE, TILE), 1)
    damp = jnp.where(row == col, DAMPING, 0.0)
    extra = count
    for p, (r, c, paired) in enumerate(table):
        block = stage[p, :TILE, :]
        if paired:
            turned = block.T
            diag = stage[0, TILE + extra : TILE + extra + 1, :]
            extra += 1
            work[r * TILE : (r + 1) * TILE, r * TILE : (r + 1) * TILE] = jnp.where(row <= col, block, turned) + damp
            second = jnp.where(row == col, diag, jnp.where(row > col, block, turned))
            work[c * TILE : (c + 1) * TILE, c * TILE : (c + 1) * TILE] = second + damp
        else:
            work[r * TILE : (r + 1) * TILE, c * TILE : (c + 1) * TILE] = block
    for b in range(count):
        rhs[:, b * TILE : (b + 1) * TILE] = full(stage[0, TILE + b : TILE + b + 1, :])
    upper_ref[...] = jnp.zeros_like(upper_ref)

    def step(b, carry):
        off = pl.multiple_of(b * TILE, TILE)
        left, right = factor_tile(work[pl.ds(off, TILE), pl.ds(off, TILE)])
        for q in range(TILE // GROUP):
            upper_ref[pl.ds(off + 8 * q, 8), pl.ds(off, TILE)] = left[q]
            inv[pl.ds(off + 8 * q, 8), :] = right[q]
        for bb in range(count):

            @pl.when(b == bb)
            def _():
                lo, hi = bb * TILE, (bb + 1) * TILE
                solved = dot_columns(rhs[:, lo:hi], inv[lo:hi, :])
                rhs[:, lo:hi] = solved
                if hi < terms:
                    panel = dot_plain(inv[lo:hi, :], work[lo:hi, hi:])
                    upper_ref[lo:hi, hi:] = panel
                    rhs[:, hi:] -= dot_plain(solved, panel)
                    for r in range(bb + 1, count):
                        s = (r - bb - 1) * TILE
                        work[r * TILE : (r + 1) * TILE, r * TILE :] -= dot_rows(panel[:, s : s + TILE], panel[:, s:])

        return carry

    lax.fori_loop(0, count, step, 0)
    for b in range(count - 1, -1, -1):
        lo, hi = b * TILE, (b + 1) * TILE
        rest = rhs[:, lo:hi]
        if hi < terms:
            rest = rest - dot_columns(rhs[:, hi:], upper_ref[lo:hi, hi:])
        rhs[:, lo:hi] = dot_plain(rest, inv[lo:hi, :])
    update = rhs[0:1, :]
    new_ref[...] = params_ref[...] + update
    gauges, doses = misfit_ref.shape
    lane = lax.broadcasted_iota(jnp.int32, (gauges, doses), 1)
    moved = jnp.zeros((gauges, doses), jnp.float32)
    for d in range(doses):
        along = jnp.sum(feat_ref[d * gauges : (d + 1) * gauges, :] * update, axis=1, keepdims=True)
        moved = jnp.where(lane == d, along, moved)
    resid_ref[...] = misfit_ref[...] - deriv_ref[...] * moved


def local(
    aerial_clips,
    basis_terms,
    holder,
    cache_slot,
    dose_index,
    dose_levels,
    threshold,
    measured,
    parameters,
):
    gauge_count = lax.axis_size("gauge")
    focus_count = lax.axis_size("focus")
    me = lax.axis_index("gauge")
    core = me & 1
    clips = aerial_clips[0]
    cached, pixels = clips.shape
    gauges = holder.shape[1]
    doses = dose_index.shape[2]
    terms = basis_terms.shape[1]
    half = pixels // 2
    step = half // CHUNKS
    gauge_bits = bits_of(gauge_count)
    offsets = list(range(0, gauge_count, 2))
    wide = gauge_bits[1:]

    notes = jnp.concatenate([holder[0], cache_slot[0], dose_index[0]], axis=1)
    both = jnp.concatenate([notes, swap(notes, "gauge", 1)], axis=0)
    relative = both[:, 0:2] ^ me
    place = relative * cached + both[:, 2:4]
    spots = jnp.arange(gauge_count * cached, dtype=jnp.int32)[None, :]
    select = (
        jnp.where(place[:, 0:1] == spots, 0.5, 0.0) + jnp.where(place[:, 1:2] == spots, 0.5, 0.0)
    ).astype(jnp.bfloat16)
    level = jnp.arange(dose_levels.shape[0], dtype=jnp.int32)
    chosen = (both[:, 4:, None] == level[None, None, :]).astype(jnp.float32)
    doses_by_gauge = STEEPNESS * jnp.sum(chosen * dose_levels[None, None, :], axis=2)

    total = None
    for k in range(CHUNKS):
        mine = lax.dynamic_slice(clips, (0, core * half + k * step), (cached, step))
        theirs = lax.dynamic_slice(clips, (0, (1 - core) * half + k * step), (cached, step))
        pieces = {0: jnp.concatenate([mine, swap(theirs, "gauge", 1)], axis=0)}
        order = wide if k % 2 == 0 else wide[::-1]
        have = [0]
        for bit in order:
            for o in list(have):
                pieces[o ^ bit] = swap(pieces[o], "gauge", bit)
                have.append(o ^ bit)
        block = (core * CHUNKS + k).astype(jnp.int32)[None]
        total = resist_rows(
            block,
            STEEPNESS * threshold,
            doses_by_gauge,
            select,
            [pieces[o] for o in offsets],
            basis_terms,
            total,
            doses,
        )
    rows = gauges * doses
    other = swap(total[rows:], "gauge", 1)

    count = terms // TILE
    table = piece_table(count)
    scale = float(rows * gauge_count * focus_count) ** (-0.5)
    slot = (me % PIECES).astype(jnp.int32)[None]
    vmem = pl.BlockSpec(memory_space=pltpu.VMEM)
    smem = pl.BlockSpec(memory_space=pltpu.SMEM)
    feat, misfit, deriv, packed = pl.pallas_call(
        functools.partial(normal_kernel, scale, table),
        grid=(1,),
        in_specs=[
            smem,
            pl.BlockSpec((rows, terms), lambda i: (0, 0)),
            pl.BlockSpec((rows, terms), lambda i: (0, 0)),
            pl.BlockSpec((gauges, doses), lambda i: (0, 0)),
            pl.BlockSpec((1, terms), lambda i: (0, 0)),
        ],
        out_specs=(
            pl.BlockSpec((rows, terms), lambda i: (0, 0)),
            pl.BlockSpec((gauges, doses), lambda i: (0, 0)),
            pl.BlockSpec((gauges, doses), lambda i: (0, 0)),
            pl.BlockSpec((PIECES, PIECE_ROWS, TILE), lambda i: (0, 0, 0)),
        ),
        out_shape=(
            jax.ShapeDtypeStruct((rows, terms), jnp.float32),
            jax.ShapeDtypeStruct((gauges, doses), jnp.float32),
            jax.ShapeDtypeStruct((gauges, doses), jnp.float32),
            jax.ShapeDtypeStruct((PIECES, PIECE_ROWS, TILE), jnp.float32),
        ),
        scratch_shapes=[pltpu.VMEM((rows, terms), jnp.float32)],
        compiler_params=pltpu.CompilerParams(vmem_limit_bytes=VMEM_BYTES),
        name="normal",
    )(slot, total, other, measured[0], parameters[None, :])

    halving, others = gauge_bits[:HALVINGS], gauge_bits[HALVINGS:]
    current = packed
    for bit in halving:
        keep = current.shape[0] // 2
        current = current[:keep] + swap(current[keep:], "gauge", bit)
    for bit in others:
        current = current + swap(current, "gauge", bit)
    for bit in bits_of(focus_count):
        current = current + swap(current, "focus", bit)
    parts = [current]
    for bit in halving[::-1]:
        parts = parts + [swap(part, "gauge", bit) for part in parts]
    groups = [[flipped(k)] for k in range(PIECES)]

    upper, new_params, residual = pl.pallas_call(
        functools.partial(factor_kernel, table, groups),
        in_specs=[smem] + [vmem] * (len(parts) + 4),
        out_specs=(vmem, vmem, vmem),
        out_shape=(
            jax.ShapeDtypeStruct((terms, terms), jnp.float32),
            jax.ShapeDtypeStruct((1, terms), jnp.float32),
            jax.ShapeDtypeStruct((gauges, doses), jnp.float32),
        ),
        scratch_shapes=[
            pltpu.VMEM((PIECES, PIECE_ROWS, TILE), jnp.float32),
            pltpu.VMEM((terms, terms), jnp.float32),
            pltpu.VMEM((terms, TILE), jnp.float32),
            pltpu.VMEM((8, terms), jnp.float32),
        ],
        compiler_params=pltpu.CompilerParams(vmem_limit_bytes=VMEM_BYTES),
        name="factor",
    )(slot, *parts, feat, misfit, deriv, parameters[None, :])
    return upper, new_params[0], residual[None]


def solution(mesh):
    return jax.shard_map(
        local,
        mesh=mesh,
        in_specs=(
            P("focus", "gauge", None),
            P(),
            P("focus", "gauge", None),
            P("focus", "gauge", None),
            P("focus", "gauge", None),
            P(),
            P("focus"),
            P("focus", "gauge", None),
            P(),
        ),
        out_specs=(P(), P(), P("focus", "gauge", None)),
        check_vma=False,
    )
```

```python
import functools

import jax
import jax.numpy as jnp
from jax import lax
from jax.experimental import pallas as pl
from jax.experimental.pallas import tpu as pltpu
from jax.sharding import PartitionSpec as P

DAMPING = 0.05
STEEPNESS = 4.0
TILE = 128
GROUP = 8
HALVINGS = 3
PIECES = 1 << HALVINGS
PIECE_ROWS = TILE + 8
CHUNKS = 4
VMEM_BYTES = 16 << 20
RESIST_BYTES = 44 << 20
VMEM = pl.BlockSpec(memory_space=pltpu.VMEM)
ANY = pl.BlockSpec(memory_space=pl.ANY)
SMEM = pl.BlockSpec(memory_space=pltpu.SMEM)
HIGHEST = lax.Precision.HIGHEST


def bits_of(size):
    return [1 << k for k in range(size.bit_length() - 1)]


def flipped(place):
    return sum(((place >> k) & 1) << (HALVINGS - 1 - k) for k in range(HALVINGS))


def swap(value, axis, bit):
    size = lax.axis_size(axis)
    return lax.ppermute(value, axis, [(i, i ^ bit) for i in range(size)])


def add_pairs(values):
    while len(values) > 1:
        values = [sum(values[i + 1 : i + 2], values[i]) for i in range(0, len(values), 2)]
    return values[0]


def exchange(value, axis, bits):
    for i in range(0, len(bits), 2):
        ways = [0]
        for bit in bits[i : i + 2]:
            ways = ways + [way | bit for way in ways]
        value = add_pairs([swap(value, axis, way) if way else value for way in ways])
    return value


def dot_rows(left, right):
    return lax.dot_general(
        left, right, (((0,), (0,)), ((), ())), precision=HIGHEST, preferred_element_type=jnp.float32
    )


def dot_plain(left, right):
    return lax.dot_general(
        left, right, (((1,), (0,)), ((), ())), precision=HIGHEST, preferred_element_type=jnp.float32
    )


def dot_columns(left, right):
    return lax.dot_general(
        left, right, (((1,), (1,)), ((), ())), precision=HIGHEST, preferred_element_type=jnp.float32
    )


def full(value):
    return jnp.broadcast_to(value, (8, TILE))


def piece_table(count):
    table = []
    for b in range(0, count, 2):
        table.append((b, b + 1, True))
    for r in range(count):
        for c in range(r + 1, count):
            table.append((r, c, False))
    return table


def resist_kernel(first, start_ref, threshold_ref, dose_ref, select_ref, *refs):
    count = len(refs) - (7 if first else 9)
    pieces, basis_ref, rest = refs[:count], refs[count], refs[count + 1 :]
    sums, outs = rest[: len(rest) - 6], rest[-6:-4]
    rows_ref, piece_buf, basis_buf, sems = rest[-4:]
    width, pixels = pieces[0].shape
    gauges, doses = dose_ref.shape[0] // 2, dose_ref.shape[1]
    start = pl.multiple_of(start_ref[0], pixels)
    copies = [
        pltpu.make_async_copy(piece, piece_buf.at[o], sems.at[o]) for o, piece in enumerate(pieces)
    ]
    fetch = pltpu.make_async_copy(basis_ref.at[pl.ds(start, pixels), :], basis_buf, sems.at[count])
    for copy in copies:
        copy.start()
    fetch.start()
    picked = None
    for o, copy in enumerate(copies):
        copy.wait()
        term = jnp.dot(
            select_ref[:, o * width : (o + 1) * width],
            piece_buf[o],
            preferred_element_type=jnp.float32,
        )
        picked = term if picked is None else picked + term
    level = threshold_ref[0]
    for d in range(doses):
        answer = jnp.tanh(dose_ref[:, d : d + 1] * picked - level).astype(jnp.bfloat16)
        for who in range(2):
            low = (who * doses + d) * gauges
            rows_ref[low : low + gauges, :] = answer[who * gauges : (who + 1) * gauges, :]
    fetch.wait()
    rows = gauges * doses
    for who in (1, 0):
        summed = jnp.dot(
            rows_ref[who * rows : (who + 1) * rows, :], basis_buf[...], preferred_element_type=jnp.float32
        )
        outs[who][...] = summed if first else sums[who][...] + summed


def resist_rows(start, threshold, dose, select, pieces, basis, totals):
    doses = dose.shape[1]
    gauges = dose.shape[0] // 2
    pair, pixels = pieces[0].shape
    terms = basis.shape[1]
    rows = gauges * doses
    first = totals is None
    operands = [dose, select, *pieces, basis] + ([] if first else list(totals))
    shape = jax.ShapeDtypeStruct((rows, terms), jnp.float32)
    return pl.pallas_call(
        functools.partial(resist_kernel, first),
        out_shape=(shape, shape),
        in_specs=[SMEM, SMEM, VMEM, VMEM] + [ANY] * (len(pieces) + 1) + [VMEM] * (0 if first else 2),
        out_specs=(VMEM, VMEM),
        scratch_shapes=[
            pltpu.VMEM((2 * rows, pixels), jnp.bfloat16),
            pltpu.VMEM((len(pieces), pair, pixels), jnp.bfloat16),
            pltpu.VMEM((pixels, terms), jnp.bfloat16),
            pltpu.SemaphoreType.DMA((len(pieces) + 1,)),
        ],
        input_output_aliases={} if first else {len(operands): 0, len(operands) + 1: 1},
        compiler_params=pltpu.CompilerParams(vmem_limit_bytes=RESIST_BYTES),
        cost_estimate=pl.CostEstimate(
            flops=4 * rows * pixels * terms,
            bytes_accessed=2 * pixels * (terms + pair * len(pieces)),
            transcendentals=2 * rows * pixels,
        ),
        name="resist",
    )(start, threshold, *operands)


def normal_kernel(scale, table, me_ref, mine_ref, other_ref, measured_ref, params_ref, feat_ref, misfit_ref, deriv_ref, keep_ref, send_ref, jac_ref):
    gauges, doses = measured_ref.shape
    terms = mine_ref.shape[1]
    count = terms // TILE
    me = me_ref[0]
    params = params_ref[...]
    lane = lax.broadcasted_iota(jnp.int32, (gauges, doses), 1)
    linear = jnp.zeros((gauges, doses), jnp.float32)
    for d in range(doses):
        low, high = d * gauges, (d + 1) * gauges
        feat = mine_ref[low:high, :] + other_ref[low:high, :]
        feat_ref[low:high, :] = feat
        along = jnp.sum(feat * params, axis=1, keepdims=True)
        linear = jnp.where(lane == d, along, linear)
    signal = jnp.tanh(linear)
    deriv = 1.0 - signal * signal
    misfit = measured_ref[...] - signal
    deriv_ref[...] = deriv
    misfit_ref[...] = misfit
    projected = jnp.zeros((1, terms), jnp.float32)
    for d in range(doses):
        low, high = d * gauges, (d + 1) * gauges
        jac = (scale * deriv[:, d : d + 1]) * feat_ref[low:high, :]
        jac_ref[low:high, :] = jac
        projected = projected + jnp.sum(jac * (scale * misfit[:, d : d + 1]), axis=0, keepdims=True)
    row = lax.broadcasted_iota(jnp.int32, (TILE, TILE), 0)
    col = lax.broadcasted_iota(jnp.int32, (TILE, TILE), 1)
    blocks = {}
    for b in range(count):
        strip = dot_rows(jac_ref[:, b * TILE : (b + 1) * TILE], jac_ref[:, b * TILE :])
        for c in range(b, count):
            blocks[b, c] = strip[:, (c - b) * TILE : (c - b + 1) * TILE]
    extra = [projected[:, b * TILE : (b + 1) * TILE] for b in range(count)]
    for r, c, paired in table:
        if paired:
            extra.append(jnp.sum(jnp.where(row == col, blocks[c, c], 0.0), axis=0, keepdims=True))
    for p, (r, c, paired) in enumerate(table):
        where = flipped(p ^ me)
        if paired:
            block = jnp.where(row <= col, blocks[r, r], blocks[c, c])
        else:
            block = blocks[r, c]
        foot = jnp.concatenate(extra + [extra[0]] * (8 - len(extra)), axis=0) if p == 0 else jnp.zeros((8, TILE), jnp.float32)
        for ref, low in ((keep_ref, 0), (send_ref, PIECES // 2)):

            @pl.when((where >= low) & (where < low + PIECES // 2))
            def _():
                ref[where - low, :TILE, :] = block
                ref[where - low, TILE:, :] = foot


def factor_tile(block):
    count = TILE // GROUP
    sub = lax.broadcasted_iota(jnp.int32, (8, TILE), 0)
    lane = lax.broadcasted_iota(jnp.int32, (8, TILE), 1)
    left = [block[8 * q : 8 * q + 8, :] for q in range(count)]
    right = [jnp.where(lane == sub + 8 * q, 1.0, 0.0).astype(jnp.float32) for q in range(count)]
    for p in range(count):
        base = GROUP * p
        cols = [full(left[p][:, base + k : base + k + 1]) for k in range(GROUP)]
        a = [[full(cols[k][m : m + 1, :]) if m >= k else None for k in range(GROUP)] for m in range(GROUP)]
        low = [[None] * GROUP for _ in range(GROUP)]
        root = []
        for k in range(GROUP):
            root.append(lax.rsqrt(a[k][k]))
            inverse = root[k] * root[k]
            for m in range(k + 1, GROUP):
                for j in range(k + 1, m + 1):
                    a[m][j] = a[m][j] - (a[m][k] * a[j][k]) * inverse
        for k in range(GROUP):
            for m in range(k + 1, GROUP):
                low[m][k] = a[m][k] * root[k]
        upper = [full(left[p][k : k + 1, :]) for k in range(GROUP)]
        other = [full(right[p][k : k + 1, :]) for k in range(GROUP)]
        for k in range(GROUP):
            upper[k] = upper[k] * root[k]
            other[k] = other[k] * root[k]
            for m in range(k + 1, GROUP):
                upper[m] = upper[m] - low[m][k] * upper[k]
                other[m] = other[m] - low[m][k] * other[k]
        for q in range(p + 1, count):
            c = [full(left[q][:, base + k : base + k + 1]) for k in range(GROUP)]
            for k in range(GROUP):
                c[k] = c[k] * root[k]
                for m in range(k + 1, GROUP):
                    c[m] = c[m] - low[m][k] * c[k]
            for k in range(GROUP):
                left[q] = left[q] - c[k] * upper[k]
                right[q] = right[q] - c[k] * other[k]
        new_left, new_right = upper[GROUP - 1], other[GROUP - 1]
        for k in range(GROUP - 1):
            new_left = jnp.where(sub == k, upper[k], new_left)
            new_right = jnp.where(sub == k, other[k], new_right)
        left[p] = jnp.where(lane >= sub + base, new_left, 0.0)
        right[p] = new_right
    return left, right


def factor_kernel(table, groups, me_ref, *refs):
    sources = refs[: len(groups)]
    feat_ref, misfit_ref, deriv_ref, params_ref, upper_ref, new_ref, resid_ref, stage, work, inv, rhs = refs[len(groups) :]
    terms = work.shape[0]
    count = terms // TILE
    me = me_ref[0]
    for source, places in zip(sources, groups):
        for k, place in enumerate(places):
            stage[place ^ me] = source[k]
    row = lax.broadcasted_iota(jnp.int32, (TILE, TILE), 0)
    col = lax.broadcasted_iota(jnp.int32, (TILE, TILE), 1)
    damp = jnp.where(row == col, DAMPING, 0.0)
    extra = count
    for p, (r, c, paired) in enumerate(table):
        block = stage[p, :TILE, :]
        if paired:
            turned = block.T
            diag = stage[0, TILE + extra : TILE + extra + 1, :]
            extra += 1
            work[r * TILE : (r + 1) * TILE, r * TILE : (r + 1) * TILE] = jnp.where(row <= col, block, turned) + damp
            second = jnp.where(row == col, diag, jnp.where(row > col, block, turned))
            work[c * TILE : (c + 1) * TILE, c * TILE : (c + 1) * TILE] = second + damp
        else:
            work[r * TILE : (r + 1) * TILE, c * TILE : (c + 1) * TILE] = block
    for b in range(count):
        rhs[:, b * TILE : (b + 1) * TILE] = full(stage[0, TILE + b : TILE + b + 1, :])
    upper_ref[...] = jnp.zeros_like(upper_ref)

    def step(b, carry):
        off = pl.multiple_of(b * TILE, TILE)
        left, right = factor_tile(work[pl.ds(off, TILE), pl.ds(off, TILE)])
        for q in range(TILE // GROUP):
            upper_ref[pl.ds(off + 8 * q, 8), pl.ds(off, TILE)] = left[q]
            inv[pl.ds(off + 8 * q, 8), :] = right[q]
        for bb in range(count):

            @pl.when(b == bb)
            def _():
                lo, hi = bb * TILE, (bb + 1) * TILE
                solved = dot_columns(rhs[:, lo:hi], inv[lo:hi, :])
                rhs[:, lo:hi] = solved
                if hi < terms:
                    panel = dot_plain(inv[lo:hi, :], work[lo:hi, hi:])
                    upper_ref[lo:hi, hi:] = panel
                    rhs[:, hi:] -= dot_plain(solved, panel)
                    for r in range(bb + 1, count):
                        s = (r - bb - 1) * TILE
                        work[r * TILE : (r + 1) * TILE, r * TILE :] -= dot_rows(panel[:, s : s + TILE], panel[:, s:])

        return carry

    lax.fori_loop(0, count, step, 0)
    for b in range(count - 1, -1, -1):
        lo, hi = b * TILE, (b + 1) * TILE
        rest = rhs[:, lo:hi]
        if hi < terms:
            rest = rest - dot_columns(rhs[:, hi:], upper_ref[lo:hi, hi:])
        rhs[:, lo:hi] = dot_plain(rest, inv[lo:hi, :])
    update = rhs[0:1, :]
    new_ref[...] = params_ref[...] + update
    gauges, doses = misfit_ref.shape
    lane = lax.broadcasted_iota(jnp.int32, (gauges, doses), 1)
    moved = jnp.zeros((gauges, doses), jnp.float32)
    for d in range(doses):
        along = jnp.sum(feat_ref[d * gauges : (d + 1) * gauges, :] * update, axis=1, keepdims=True)
        moved = jnp.where(lane == d, along, moved)
    resid_ref[...] = misfit_ref[...] - deriv_ref[...] * moved


def local(
    aerial_clips,
    basis_terms,
    holder,
    cache_slot,
    dose_index,
    dose_levels,
    threshold,
    measured,
    parameters,
):
    gauge_count = lax.axis_size("gauge")
    focus_count = lax.axis_size("focus")
    me = lax.axis_index("gauge")
    core = me & 1
    clips = aerial_clips[0]
    cached, pixels = clips.shape
    gauges = holder.shape[1]
    doses = dose_index.shape[2]
    terms = basis_terms.shape[1]
    half = pixels // 2
    step = half // CHUNKS
    gauge_bits = bits_of(gauge_count)
    offsets = list(range(0, gauge_count, 2))
    wide = gauge_bits[1:]

    notes = jnp.concatenate([holder[0], cache_slot[0], dose_index[0]], axis=1)
    theirs_notes = swap(notes, "gauge", 1)
    chunks = []
    for k in range(CHUNKS):
        if k == 1:
            clips, chunks[0][0] = lax.optimization_barrier((clips, chunks[0][0]))
        mine = lax.dynamic_slice(clips, (0, core * half + k * step), (cached, step))
        theirs = lax.dynamic_slice(clips, (0, (1 - core) * half + k * step), (cached, step))
        block = jnp.concatenate([mine, swap(theirs, "gauge", 1)], axis=0)
        order = wide if k % 2 == 0 else wide[::-1]
        if k > 1:
            before = chunks[k - 2]
            block, before[order[0]] = lax.optimization_barrier((block, before[order[0]]))
        pieces, have = {0: block}, [0]
        for bit in order:
            for o in list(have):
                pieces[o ^ bit] = swap(pieces[o], "gauge", bit)
                have.append(o ^ bit)
        chunks.append(pieces)

    def orders(own, values):
        relative = values[:, 0:2] ^ own
        place = relative * cached + values[:, 2:4]
        spots = jnp.arange(gauge_count * cached, dtype=jnp.int32)[None, :]
        select = jnp.where(place[:, 0:1] == spots, 0.5, 0.0) + jnp.where(place[:, 1:2] == spots, 0.5, 0.0)
        level = jnp.arange(dose_levels.shape[0], dtype=jnp.int32)
        chosen = (values[:, 4:, None] == level[None, None, :]).astype(jnp.float32)
        return STEEPNESS * jnp.sum(chosen * dose_levels[None, None, :], axis=2), select.astype(jnp.bfloat16)

    anchor = chunks[0][wide[0]]
    notes, theirs_notes, anchor = lax.optimization_barrier((notes, theirs_notes, anchor))
    chunks[0][wide[0]] = anchor
    mine_orders, their_orders = orders(me, notes), orders(me, theirs_notes)
    dose, select = [jnp.concatenate(both, axis=0) for both in zip(mine_orders, their_orders)]
    level = STEEPNESS * threshold
    totals = None
    for k in range(CHUNKS):
        start = (core * half + k * step).astype(jnp.int32)[None]
        held = [chunks[k][o] for o in offsets]
        totals = resist_rows(start, level, dose, select, held, basis_terms, totals)
    mine_total, their_total = totals
    rows = gauges * doses
    other = swap(their_total, "gauge", 1)

    count = terms // TILE
    table = piece_table(count)
    scale = float(rows * gauge_count * focus_count) ** (-0.5)
    slot = (me % PIECES).astype(jnp.int32)[None]
    feat, misfit, deriv, kept, sent = pl.pallas_call(
        functools.partial(normal_kernel, scale, table),
        in_specs=[SMEM] + [VMEM] * 4,
        out_specs=(VMEM,) * 5,
        out_shape=(
            jax.ShapeDtypeStruct((rows, terms), jnp.float32),
            jax.ShapeDtypeStruct((gauges, doses), jnp.float32),
            jax.ShapeDtypeStruct((gauges, doses), jnp.float32),
            jax.ShapeDtypeStruct((PIECES // 2, PIECE_ROWS, TILE), jnp.float32),
            jax.ShapeDtypeStruct((PIECES // 2, PIECE_ROWS, TILE), jnp.float32),
        ),
        scratch_shapes=[pltpu.VMEM((rows, terms), jnp.float32)],
        compiler_params=pltpu.CompilerParams(vmem_limit_bytes=VMEM_BYTES),
        name="normal",
    )(slot, mine_total, other, measured[0], parameters[None, :])

    first, near, others = gauge_bits[0], gauge_bits[1:HALVINGS], gauge_bits[HALVINGS:]
    ways = [sum(bit for n, bit in enumerate(near) if (p >> (len(near) - 1 - n)) & 1) for p in range(PIECES // 2)]
    got = swap(sent, "gauge", first)
    parts = [kept[p : p + 1] + got[p : p + 1] for p in range(PIECES // 2)]
    terms_in = [parts[0]] + [swap(parts[p], "gauge", ways[p]) for p in range(1, PIECES // 2)]
    current = add_pairs(terms_in)
    current = exchange(current, "gauge", others)
    current = exchange(current, "focus", bits_of(focus_count))
    parts = [current] + [swap(current, "gauge", way) for way in ways[1:]]
    parts = parts + [swap(part, "gauge", first) for part in parts]
    order = list(range(PIECES))
    groups = [[flipped(k)] for k in order]

    upper, new_params, residual = pl.pallas_call(
        functools.partial(factor_kernel, table, groups),
        in_specs=[SMEM] + [VMEM] * (len(parts) + 4),
        out_specs=(VMEM, VMEM, VMEM),
        out_shape=(
            jax.ShapeDtypeStruct((terms, terms), jnp.float32),
            jax.ShapeDtypeStruct((1, terms), jnp.float32),
            jax.ShapeDtypeStruct((gauges, doses), jnp.float32),
        ),
        scratch_shapes=[
            pltpu.VMEM((PIECES, PIECE_ROWS, TILE), jnp.float32),
            pltpu.VMEM((terms, terms), jnp.float32),
            pltpu.VMEM((terms, TILE), jnp.float32),
            pltpu.VMEM((8, terms), jnp.float32),
        ],
        compiler_params=pltpu.CompilerParams(vmem_limit_bytes=VMEM_BYTES),
        name="factor",
    )(slot, *parts, feat, misfit, deriv, parameters[None, :])
    return upper, new_params[0], residual[None]


def solution(mesh):
    return jax.shard_map(
        local,
        mesh=mesh,
        in_specs=(
            P("focus", "gauge", None),
            P(),
            P("focus", "gauge", None),
            P("focus", "gauge", None),
            P("focus", "gauge", None),
            P(),
            P("focus"),
            P("focus", "gauge", None),
            P(),
        ),
        out_specs=(P(), P(), P("focus", "gauge", None)),
        check_vma=False,
    )
```

```python
import functools

import jax
import jax.numpy as jnp
from jax import lax
from jax.experimental import pallas as pl
from jax.experimental.pallas import tpu as pltpu
from jax.sharding import PartitionSpec as P

DAMPING = 0.05
STEEPNESS = 4.0
TILE = 128
GROUP = 8
HALVINGS = 3
PIECES = 1 << HALVINGS
PIECE_ROWS = TILE + 8
CHUNKS = 4
TOGETHER = 2
VMEM_BYTES = 16 << 20
RESIST_BYTES = 44 << 20
VMEM = pl.BlockSpec(memory_space=pltpu.VMEM)
ANY = pl.BlockSpec(memory_space=pl.ANY)
SMEM = pl.BlockSpec(memory_space=pltpu.SMEM)
HIGHEST = lax.Precision.HIGHEST


def bits_of(size):
    return [1 << k for k in range(size.bit_length() - 1)]


def flipped(place):
    return sum(((place >> k) & 1) << (HALVINGS - 1 - k) for k in range(HALVINGS))


def swap(value, axis, bit):
    size = lax.axis_size(axis)
    return lax.ppermute(value, axis, [(i, i ^ bit) for i in range(size)])


def add_pairs(values):
    while len(values) > 1:
        values = [sum(values[i + 1 : i + 2], values[i]) for i in range(0, len(values), 2)]
    return values[0]


def exchange(value, axis, bits):
    for i in range(0, len(bits), 2):
        ways = [0]
        for bit in bits[i : i + 2]:
            ways = ways + [way | bit for way in ways]
        value = add_pairs([swap(value, axis, way) if way else value for way in ways])
    return value


def dot_rows(left, right):
    return lax.dot_general(
        left, right, (((0,), (0,)), ((), ())), precision=HIGHEST, preferred_element_type=jnp.float32
    )


def dot_plain(left, right):
    return lax.dot_general(
        left, right, (((1,), (0,)), ((), ())), precision=HIGHEST, preferred_element_type=jnp.float32
    )


def dot_columns(left, right):
    return lax.dot_general(
        left, right, (((1,), (1,)), ((), ())), precision=HIGHEST, preferred_element_type=jnp.float32
    )


def full(value):
    return jnp.broadcast_to(value, (8, TILE))


def piece_table(count):
    table = []
    for b in range(0, count, 2):
        table.append((b, b + 1, True))
    for r in range(count):
        for c in range(r + 1, count):
            table.append((r, c, False))
    return table


def resist_kernel(first, start_ref, threshold_ref, dose_ref, select_ref, *refs):
    count = len(refs) - (7 if first else 9)
    pieces, basis_ref, rest = refs[:count], refs[count], refs[count + 1 :]
    sums, outs = rest[: len(rest) - 6], rest[-6:-4]
    rows_ref, piece_buf, basis_buf, sems = rest[-4:]
    width, pixels = pieces[0].shape
    each = select_ref.shape[1] // width
    gauges, doses = dose_ref.shape[0] // 2, dose_ref.shape[1]
    taken = basis_buf.shape[0]
    start = pl.multiple_of(start_ref[0], pixels)
    copies = [
        pltpu.make_async_copy(piece, piece_buf.at[at], sems.at[at]) for at, piece in enumerate(pieces)
    ]
    fetch = pltpu.make_async_copy(basis_ref.at[pl.ds(start, taken), :], basis_buf, sems.at[count])
    for copy in copies:
        copy.start()
    fetch.start()
    level = threshold_ref[0]
    for g in range(count // each):
        for copy in copies[g * each : (g + 1) * each]:
            copy.wait()
        if (g + 1) * each == count:
            fetch.wait()
        picked = None
        for o in range(each):
            term = jnp.dot(
                select_ref[:, o * width : (o + 1) * width],
                piece_buf[g * each + o],
                preferred_element_type=jnp.float32,
            )
            picked = term if picked is None else picked + term
        for d in range(doses):
            answer = jnp.tanh(dose_ref[:, d : d + 1] * picked - level).astype(jnp.bfloat16)
            for who in range(2):
                low = (who * doses + d) * gauges
                rows_ref[low : low + gauges, g * pixels : (g + 1) * pixels] = answer[
                    who * gauges : (who + 1) * gauges, :
                ]
    rows = gauges * doses
    for who in (1, 0):
        summed = jnp.dot(
            rows_ref[who * rows : (who + 1) * rows, :], basis_buf[...], preferred_element_type=jnp.float32
        )
        outs[who][...] = summed if first else sums[who][...] + summed


def resist_rows(start, threshold, dose, select, pieces, basis, totals):
    doses = dose.shape[1]
    gauges = dose.shape[0] // 2
    pair, pixels = pieces[0].shape
    terms = basis.shape[1]
    rows = gauges * doses
    taken = pixels * len(pieces) * pair // select.shape[1]
    first = totals is None
    operands = [dose, select, *pieces, basis] + ([] if first else list(totals))
    shape = jax.ShapeDtypeStruct((rows, terms), jnp.float32)
    return pl.pallas_call(
        functools.partial(resist_kernel, first),
        out_shape=(shape, shape),
        in_specs=[SMEM, SMEM, VMEM, VMEM] + [ANY] * (len(pieces) + 1) + [VMEM] * (0 if first else 2),
        out_specs=(VMEM, VMEM),
        scratch_shapes=[
            pltpu.VMEM((2 * rows, taken), jnp.bfloat16),
            pltpu.VMEM((len(pieces), pair, pixels), jnp.bfloat16),
            pltpu.VMEM((taken, terms), jnp.bfloat16),
            pltpu.SemaphoreType.DMA((len(pieces) + 1,)),
        ],
        input_output_aliases={} if first else {len(operands): 0, len(operands) + 1: 1},
        compiler_params=pltpu.CompilerParams(vmem_limit_bytes=RESIST_BYTES),
        cost_estimate=pl.CostEstimate(
            flops=4 * rows * taken * terms,
            bytes_accessed=2 * taken * (terms + select.shape[1]),
            transcendentals=2 * rows * taken,
        ),
        name="resist",
    )(start, threshold, *operands)


def normal_kernel(scale, table, me_ref, mine_ref, other_ref, measured_ref, params_ref, feat_ref, misfit_ref, deriv_ref, keep_ref, send_ref, jac_ref):
    gauges, doses = measured_ref.shape
    terms = mine_ref.shape[1]
    count = terms // TILE
    me = me_ref[0]
    params = params_ref[...]
    lane = lax.broadcasted_iota(jnp.int32, (gauges, doses), 1)
    linear = jnp.zeros((gauges, doses), jnp.float32)
    for d in range(doses):
        low, high = d * gauges, (d + 1) * gauges
        feat = mine_ref[low:high, :] + other_ref[low:high, :]
        feat_ref[low:high, :] = feat
        along = jnp.sum(feat * params, axis=1, keepdims=True)
        linear = jnp.where(lane == d, along, linear)
    signal = jnp.tanh(linear)
    deriv = 1.0 - signal * signal
    misfit = measured_ref[...] - signal
    deriv_ref[...] = deriv
    misfit_ref[...] = misfit
    projected = jnp.zeros((1, terms), jnp.float32)
    for d in range(doses):
        low, high = d * gauges, (d + 1) * gauges
        jac = (scale * deriv[:, d : d + 1]) * feat_ref[low:high, :]
        jac_ref[low:high, :] = jac
        projected = projected + jnp.sum(jac * (scale * misfit[:, d : d + 1]), axis=0, keepdims=True)
    row = lax.broadcasted_iota(jnp.int32, (TILE, TILE), 0)
    col = lax.broadcasted_iota(jnp.int32, (TILE, TILE), 1)
    blocks = {}
    for b in range(count):
        strip = dot_rows(jac_ref[:, b * TILE : (b + 1) * TILE], jac_ref[:, b * TILE :])
        for c in range(b, count):
            blocks[b, c] = strip[:, (c - b) * TILE : (c - b + 1) * TILE]
    extra = [projected[:, b * TILE : (b + 1) * TILE] for b in range(count)]
    for r, c, paired in table:
        if paired:
            extra.append(jnp.sum(jnp.where(row == col, blocks[c, c], 0.0), axis=0, keepdims=True))
    for p, (r, c, paired) in enumerate(table):
        where = flipped(p ^ me)
        if paired:
            block = jnp.where(row <= col, blocks[r, r], blocks[c, c])
        else:
            block = blocks[r, c]
        foot = jnp.concatenate(extra + [extra[0]] * (8 - len(extra)), axis=0) if p == 0 else jnp.zeros((8, TILE), jnp.float32)
        for ref, low in ((keep_ref, 0), (send_ref, PIECES // 2)):

            @pl.when((where >= low) & (where < low + PIECES // 2))
            def _():
                ref[where - low, :TILE, :] = block
                ref[where - low, TILE:, :] = foot


def factor_tile(block, cols_ref, ahead_ref):
    count = TILE // GROUP
    sub = lax.broadcasted_iota(jnp.int32, (8, TILE), 0)
    lane = lax.broadcasted_iota(jnp.int32, (8, TILE), 1)
    left = [block[8 * q : 8 * q + 8, :] for q in range(count)]
    right = [jnp.where(lane == sub + 8 * q, 1.0, 0.0).astype(jnp.float32) for q in range(count)]
    cols = [full(left[0][:, k : k + 1]) for k in range(GROUP)]
    for p in range(count):
        base = GROUP * p
        corner = 64 * p
        for k in range(GROUP):
            cols_ref[corner + 8 * k : corner + 8 * k + 8, :] = cols[k]
        a = [
            [cols_ref[pl.ds(corner + 8 * k + m, 8, stride=0), :] if m >= k else None for k in range(GROUP)]
            for m in range(GROUP)
        ]
        if p + 1 < count:
            cols = [full(left[p + 1][:, base + 8 + k : base + 9 + k]) for k in range(GROUP)]
        low = [[None] * GROUP for _ in range(GROUP)]
        root = []
        for k in range(GROUP):
            root.append(lax.rsqrt(a[k][k]))
            inverse = root[k] * root[k]
            for m in range(k + 1, GROUP):
                for j in range(k + 1, m + 1):
                    a[m][j] = a[m][j] - (a[m][k] * a[j][k]) * inverse
        for k in range(GROUP):
            for m in range(k + 1, GROUP):
                low[m][k] = a[m][k] * root[k]
        upper = [full(left[p][k : k + 1, :]) for k in range(GROUP)]
        other = [full(right[p][k : k + 1, :]) for k in range(GROUP)]
        for k in range(GROUP):
            upper[k] = upper[k] * root[k]
            other[k] = other[k] * root[k]
            for m in range(k + 1, GROUP):
                upper[m] = upper[m] - low[m][k] * upper[k]
                other[m] = other[m] - low[m][k] * other[k]
        for q in range(p + 1, count):
            c = [full(left[q][:, base + k : base + k + 1]) for k in range(GROUP)]
            for k in range(GROUP):
                c[k] = c[k] * root[k]
                for m in range(k + 1, GROUP):
                    c[m] = c[m] - low[m][k] * c[k]
            if q == p + 1:
                for k in range(GROUP):
                    ahead_ref[corner + 8 * k : corner + 8 * k + 8, :] = c[k]
                for m in range(GROUP):
                    for k in range(GROUP):
                        cols[m] = cols[m] - c[k] * ahead_ref[pl.ds(corner + 8 * k + m, 8, stride=0), :]
            for k in range(GROUP):
                left[q] = left[q] - c[k] * upper[k]
                right[q] = right[q] - c[k] * other[k]
        new_left, new_right = upper[GROUP - 1], other[GROUP - 1]
        for k in range(GROUP - 1):
            new_left = jnp.where(sub == k, upper[k], new_left)
            new_right = jnp.where(sub == k, other[k], new_right)
        left[p] = jnp.where(lane >= sub + base, new_left, 0.0)
        right[p] = new_right
    return left, right


def factor_kernel(table, groups, me_ref, *refs):
    sources = refs[: len(groups)]
    feat_ref, misfit_ref, deriv_ref, params_ref, upper_ref, new_ref, resid_ref, stage, work, inv, rhs, cols_ref, ahead_ref = refs[len(groups) :]
    terms = work.shape[0]
    count = terms // TILE
    me = me_ref[0]
    for source, places in zip(sources, groups):
        for k, place in enumerate(places):
            stage[place ^ me] = source[k]
    row = lax.broadcasted_iota(jnp.int32, (TILE, TILE), 0)
    col = lax.broadcasted_iota(jnp.int32, (TILE, TILE), 1)
    damp = jnp.where(row == col, DAMPING, 0.0)
    extra = count
    for p, (r, c, paired) in enumerate(table):
        block = stage[p, :TILE, :]
        if paired:
            turned = block.T
            diag = stage[0, TILE + extra : TILE + extra + 1, :]
            extra += 1
            work[r * TILE : (r + 1) * TILE, r * TILE : (r + 1) * TILE] = jnp.where(row <= col, block, turned) + damp
            second = jnp.where(row == col, diag, jnp.where(row > col, block, turned))
            work[c * TILE : (c + 1) * TILE, c * TILE : (c + 1) * TILE] = second + damp
        else:
            work[r * TILE : (r + 1) * TILE, c * TILE : (c + 1) * TILE] = block
    for b in range(count):
        rhs[:, b * TILE : (b + 1) * TILE] = full(stage[0, TILE + b : TILE + b + 1, :])
    upper_ref[...] = jnp.zeros_like(upper_ref)

    def step(b, carry):
        off = pl.multiple_of(b * TILE, TILE)
        left, right = factor_tile(work[pl.ds(off, TILE), pl.ds(off, TILE)], cols_ref, ahead_ref)
        for q in range(TILE // GROUP):
            upper_ref[pl.ds(off + 8 * q, 8), pl.ds(off, TILE)] = left[q]
            inv[pl.ds(off + 8 * q, 8), :] = right[q]
        for bb in range(count):

            @pl.when(b == bb)
            def _():
                lo, hi = bb * TILE, (bb + 1) * TILE
                solved = dot_columns(rhs[:, lo:hi], inv[lo:hi, :])
                rhs[:, lo:hi] = solved
                if hi < terms:
                    panel = dot_plain(inv[lo:hi, :], work[lo:hi, hi:])
                    upper_ref[lo:hi, hi:] = panel
                    rhs[:, hi:] -= dot_plain(solved, panel)
                    for r in range(bb + 1, count):
                        s = (r - bb - 1) * TILE
                        work[r * TILE : (r + 1) * TILE, r * TILE :] -= dot_rows(panel[:, s : s + TILE], panel[:, s:])

        return carry

    lax.fori_loop(0, count, step, 0)
    for b in range(count - 1, -1, -1):
        lo, hi = b * TILE, (b + 1) * TILE
        rest = rhs[:, lo:hi]
        if hi < terms:
            rest = rest - dot_columns(rhs[:, hi:], upper_ref[lo:hi, hi:])
        rhs[:, lo:hi] = dot_plain(rest, inv[lo:hi, :])
    update = rhs[0:1, :]
    new_ref[...] = params_ref[...] + update
    gauges, doses = misfit_ref.shape
    lane = lax.broadcasted_iota(jnp.int32, (gauges, doses), 1)
    moved = jnp.zeros((gauges, doses), jnp.float32)
    for d in range(doses):
        along = jnp.sum(feat_ref[d * gauges : (d + 1) * gauges, :] * update, axis=1, keepdims=True)
        moved = jnp.where(lane == d, along, moved)
    resid_ref[...] = misfit_ref[...] - deriv_ref[...] * moved


def local(
    aerial_clips,
    basis_terms,
    holder,
    cache_slot,
    dose_index,
    dose_levels,
    threshold,
    measured,
    parameters,
):
    gauge_count = lax.axis_size("gauge")
    focus_count = lax.axis_size("focus")
    me = lax.axis_index("gauge")
    core = me & 1
    clips = aerial_clips[0]
    cached, pixels = clips.shape
    gauges = holder.shape[1]
    doses = dose_index.shape[2]
    terms = basis_terms.shape[1]
    half = pixels // 2
    step = half // CHUNKS
    gauge_bits = bits_of(gauge_count)
    offsets = list(range(0, gauge_count, 2))
    wide = gauge_bits[1:]

    notes = jnp.concatenate([holder[0], cache_slot[0], dose_index[0]], axis=1)
    theirs_notes = swap(notes, "gauge", 1)
    chunks = []
    for k in range(CHUNKS):
        if k == 1:
            clips, chunks[0][0] = lax.optimization_barrier((clips, chunks[0][0]))
        mine = lax.dynamic_slice(clips, (0, core * half + k * step), (cached, step))
        theirs = lax.dynamic_slice(clips, (0, (1 - core) * half + k * step), (cached, step))
        block = jnp.concatenate([mine, swap(theirs, "gauge", 1)], axis=0)
        order = wide if k % 2 == 0 else wide[::-1]
        if k > 1:
            before = chunks[k - 2]
            block, before[order[0]] = lax.optimization_barrier((block, before[order[0]]))
        pieces, have = {0: block}, [0]
        for bit in order:
            for o in list(have):
                pieces[o ^ bit] = swap(pieces[o], "gauge", bit)
                have.append(o ^ bit)
        chunks.append(pieces)

    def orders(own, values):
        relative = values[:, 0:2] ^ own
        place = relative * cached + values[:, 2:4]
        spots = jnp.arange(gauge_count * cached, dtype=jnp.int32)[None, :]
        select = jnp.where(place[:, 0:1] == spots, 0.5, 0.0) + jnp.where(place[:, 1:2] == spots, 0.5, 0.0)
        level = jnp.arange(dose_levels.shape[0], dtype=jnp.int32)
        chosen = (values[:, 4:, None] == level[None, None, :]).astype(jnp.float32)
        return STEEPNESS * jnp.sum(chosen * dose_levels[None, None, :], axis=2), select.astype(jnp.bfloat16)

    anchor = chunks[0][wide[0]]
    notes, theirs_notes, anchor = lax.optimization_barrier((notes, theirs_notes, anchor))
    chunks[0][wide[0]] = anchor
    mine_orders, their_orders = orders(me, notes), orders(me, theirs_notes)
    dose, select = [jnp.concatenate(both, axis=0) for both in zip(mine_orders, their_orders)]
    level = STEEPNESS * threshold
    totals = None
    for k in range(0, CHUNKS, TOGETHER):
        start = (core * half + k * step).astype(jnp.int32)[None]
        held = [chunk[o] for chunk in chunks[k : k + TOGETHER] for o in offsets]
        totals = resist_rows(start, level, dose, select, held, basis_terms, totals)
    mine_total, their_total = totals
    rows = gauges * doses
    other = swap(their_total, "gauge", 1)

    count = terms // TILE
    table = piece_table(count)
    scale = float(rows * gauge_count * focus_count) ** (-0.5)
    slot = (me % PIECES).astype(jnp.int32)[None]
    feat, misfit, deriv, kept, sent = pl.pallas_call(
        functools.partial(normal_kernel, scale, table),
        in_specs=[SMEM] + [VMEM] * 4,
        out_specs=(VMEM,) * 5,
        out_shape=(
            jax.ShapeDtypeStruct((rows, terms), jnp.float32),
            jax.ShapeDtypeStruct((gauges, doses), jnp.float32),
            jax.ShapeDtypeStruct((gauges, doses), jnp.float32),
            jax.ShapeDtypeStruct((PIECES // 2, PIECE_ROWS, TILE), jnp.float32),
            jax.ShapeDtypeStruct((PIECES // 2, PIECE_ROWS, TILE), jnp.float32),
        ),
        scratch_shapes=[pltpu.VMEM((rows, terms), jnp.float32)],
        compiler_params=pltpu.CompilerParams(vmem_limit_bytes=VMEM_BYTES),
        name="normal",
    )(slot, mine_total, other, measured[0], parameters[None, :])

    first, near, others = gauge_bits[0], gauge_bits[1:HALVINGS], gauge_bits[HALVINGS:]
    ways = [sum(bit for n, bit in enumerate(near) if (p >> (len(near) - 1 - n)) & 1) for p in range(PIECES // 2)]
    got = swap(sent, "gauge", first)
    parts = [kept[p : p + 1] + got[p : p + 1] for p in range(PIECES // 2)]
    terms_in = [parts[0]] + [swap(parts[p], "gauge", ways[p]) for p in range(1, PIECES // 2)]
    current = add_pairs(terms_in)
    current = exchange(current, "gauge", others)
    current = exchange(current, "focus", bits_of(focus_count))
    parts = [current] + [swap(current, "gauge", way) for way in ways[1:]]
    parts = parts + [swap(part, "gauge", first) for part in parts]
    order = list(range(PIECES))
    groups = [[flipped(k)] for k in order]

    upper, new_params, residual = pl.pallas_call(
        functools.partial(factor_kernel, table, groups),
        in_specs=[SMEM] + [VMEM] * (len(parts) + 4),
        out_specs=(VMEM, VMEM, VMEM),
        out_shape=(
            jax.ShapeDtypeStruct((terms, terms), jnp.float32),
            jax.ShapeDtypeStruct((1, terms), jnp.float32),
            jax.ShapeDtypeStruct((gauges, doses), jnp.float32),
        ),
        scratch_shapes=[
            pltpu.VMEM((PIECES, PIECE_ROWS, TILE), jnp.float32),
            pltpu.VMEM((terms, terms), jnp.float32),
            pltpu.VMEM((terms, TILE), jnp.float32),
            pltpu.VMEM((8, terms), jnp.float32),
            pltpu.VMEM((TILE * GROUP, TILE), jnp.float32),
            pltpu.VMEM((TILE * GROUP, TILE), jnp.float32),
        ],
        compiler_params=pltpu.CompilerParams(vmem_limit_bytes=VMEM_BYTES),
        name="factor",
    )(slot, *parts, feat, misfit, deriv, parameters[None, :])
    return upper, new_params[0], residual[None]


def solution(mesh):
    return jax.shard_map(
        local,
        mesh=mesh,
        in_specs=(
            P("focus", "gauge", None),
            P(),
            P("focus", "gauge", None),
            P("focus", "gauge", None),
            P("focus", "gauge", None),
            P(),
            P("focus"),
            P("focus", "gauge", None),
            P(),
        ),
        out_specs=(P(), P(), P("focus", "gauge", None)),
        check_vma=False,
    )
```

```python
import functools

import jax
import jax.numpy as jnp
from jax import lax
from jax.experimental import pallas as pl
from jax.experimental.pallas import tpu as pltpu
from jax.sharding import PartitionSpec as P

DAMPING = 0.05
STEEPNESS = 4.0
TILE = 128
GROUP = 8
HALVINGS = 3
PIECES = 1 << HALVINGS
PIECE_ROWS = TILE + 8
CHUNKS = 4
TOGETHER = 2
VMEM_BYTES = 16 << 20
RESIST_BYTES = 44 << 20
VMEM = pl.BlockSpec(memory_space=pltpu.VMEM)
ANY = pl.BlockSpec(memory_space=pl.ANY)
SMEM = pl.BlockSpec(memory_space=pltpu.SMEM)
HIGHEST = lax.Precision.HIGHEST


def bits_of(size):
    return [1 << k for k in range(size.bit_length() - 1)]


def flipped(place):
    return sum(((place >> k) & 1) << (HALVINGS - 1 - k) for k in range(HALVINGS))


def swap(value, axis, bit):
    size = lax.axis_size(axis)
    return lax.ppermute(value, axis, [(i, i ^ bit) for i in range(size)])


def add_pairs(values):
    while len(values) > 1:
        values = [sum(values[i + 1 : i + 2], values[i]) for i in range(0, len(values), 2)]
    return values[0]


def exchange(value, axis, bits):
    for i in range(0, len(bits), 2):
        ways = [0]
        for bit in bits[i : i + 2]:
            ways = ways + [way | bit for way in ways]
        value = add_pairs([swap(value, axis, way) if way else value for way in ways])
    return value


def dot_rows(left, right):
    return lax.dot_general(
        left, right, (((0,), (0,)), ((), ())), precision=HIGHEST, preferred_element_type=jnp.float32
    )


def dot_plain(left, right):
    return lax.dot_general(
        left, right, (((1,), (0,)), ((), ())), precision=HIGHEST, preferred_element_type=jnp.float32
    )


def dot_columns(left, right):
    return lax.dot_general(
        left, right, (((1,), (1,)), ((), ())), precision=HIGHEST, preferred_element_type=jnp.float32
    )


def halves(value):
    high = value.astype(jnp.bfloat16)
    return high, (value - high.astype(jnp.float32)).astype(jnp.bfloat16)


def dot_halves(left, right):
    dot = lambda a, b: lax.dot_general(a, b, (((0,), (0,)), ((), ())), preferred_element_type=jnp.float32)
    return dot(left[0], right[0]) + (dot(left[0], right[1]) + dot(left[1], right[0]))


def full(value):
    return jnp.broadcast_to(value, (8, TILE))


def piece_table(count):
    table = []
    for b in range(0, count, 2):
        table.append((b, b + 1, True))
    for r in range(count):
        for c in range(r + 1, count):
            table.append((r, c, False))
    return table


def resist_kernel(first, start_ref, threshold_ref, dose_ref, select_ref, *refs):
    count = len(refs) - (7 if first else 9)
    pieces, basis_ref, rest = refs[:count], refs[count], refs[count + 1 :]
    sums, outs = rest[: len(rest) - 6], rest[-6:-4]
    rows_ref, piece_buf, basis_buf, sems = rest[-4:]
    width, pixels = pieces[0].shape
    each = select_ref.shape[1] // width
    gauges, doses = dose_ref.shape[0] // 2, dose_ref.shape[1]
    taken = basis_buf.shape[0]
    start = pl.multiple_of(start_ref[0], pixels)
    copies = [
        pltpu.make_async_copy(piece, piece_buf.at[at], sems.at[at]) for at, piece in enumerate(pieces)
    ]
    fetch = pltpu.make_async_copy(basis_ref.at[pl.ds(start, taken), :], basis_buf, sems.at[count])
    for copy in copies:
        copy.start()
    fetch.start()
    level = threshold_ref[0]
    for g in range(count // each):
        for copy in copies[g * each : (g + 1) * each]:
            copy.wait()
        if (g + 1) * each == count:
            fetch.wait()
        picked = None
        for o in range(each):
            term = jnp.dot(
                select_ref[:, o * width : (o + 1) * width],
                piece_buf[g * each + o],
                preferred_element_type=jnp.float32,
            )
            picked = term if picked is None else picked + term
        for d in range(doses):
            answer = jnp.tanh(dose_ref[:, d : d + 1] * picked - level).astype(jnp.bfloat16)
            for who in range(2):
                low = (who * doses + d) * gauges
                rows_ref[low : low + gauges, g * pixels : (g + 1) * pixels] = answer[
                    who * gauges : (who + 1) * gauges, :
                ]
    rows = gauges * doses
    for who in (1, 0):
        summed = jnp.dot(
            rows_ref[who * rows : (who + 1) * rows, :], basis_buf[...], preferred_element_type=jnp.float32
        )
        outs[who][...] = summed if first else sums[who][...] + summed


def resist_rows(start, threshold, dose, select, pieces, basis, totals):
    doses = dose.shape[1]
    gauges = dose.shape[0] // 2
    pair, pixels = pieces[0].shape
    terms = basis.shape[1]
    rows = gauges * doses
    taken = pixels * len(pieces) * pair // select.shape[1]
    first = totals is None
    operands = [dose, select, *pieces, basis] + ([] if first else list(totals))
    shape = jax.ShapeDtypeStruct((rows, terms), jnp.float32)
    return pl.pallas_call(
        functools.partial(resist_kernel, first),
        out_shape=(shape, shape),
        in_specs=[SMEM, SMEM, VMEM, VMEM] + [ANY] * (len(pieces) + 1) + [VMEM] * (0 if first else 2),
        out_specs=(VMEM, VMEM),
        scratch_shapes=[
            pltpu.VMEM((2 * rows, taken), jnp.bfloat16),
            pltpu.VMEM((len(pieces), pair, pixels), jnp.bfloat16),
            pltpu.VMEM((taken, terms), jnp.bfloat16),
            pltpu.SemaphoreType.DMA((len(pieces) + 1,)),
        ],
        input_output_aliases={} if first else {len(operands): 0, len(operands) + 1: 1},
        compiler_params=pltpu.CompilerParams(vmem_limit_bytes=RESIST_BYTES),
        cost_estimate=pl.CostEstimate(
            flops=4 * rows * taken * terms,
            bytes_accessed=2 * taken * (terms + select.shape[1]),
            transcendentals=2 * rows * taken,
        ),
        name="resist",
    )(start, threshold, *operands)


def normal_kernel(scale, table, me_ref, mine_ref, other_ref, measured_ref, params_ref, feat_ref, misfit_ref, deriv_ref, keep_ref, send_ref, jac_ref):
    gauges, doses = measured_ref.shape
    terms = mine_ref.shape[1]
    count = terms // TILE
    me = me_ref[0]
    params = params_ref[...]
    lane = lax.broadcasted_iota(jnp.int32, (gauges, doses), 1)
    linear = jnp.zeros((gauges, doses), jnp.float32)
    for d in range(doses):
        low, high = d * gauges, (d + 1) * gauges
        feat = mine_ref[low:high, :] + other_ref[low:high, :]
        feat_ref[low:high, :] = feat
        along = jnp.sum(feat * params, axis=1, keepdims=True)
        linear = jnp.where(lane == d, along, linear)
    signal = jnp.tanh(linear)
    deriv = 1.0 - signal * signal
    misfit = measured_ref[...] - signal
    deriv_ref[...] = deriv
    misfit_ref[...] = misfit
    projected = jnp.zeros((1, terms), jnp.float32)
    for d in range(doses):
        low, high = d * gauges, (d + 1) * gauges
        jac = (scale * deriv[:, d : d + 1]) * feat_ref[low:high, :]
        jac_ref[low:high, :] = jac
        projected = projected + jnp.sum(jac * (scale * misfit[:, d : d + 1]), axis=0, keepdims=True)
    row = lax.broadcasted_iota(jnp.int32, (TILE, TILE), 0)
    col = lax.broadcasted_iota(jnp.int32, (TILE, TILE), 1)
    blocks = {}
    high, low = halves(jac_ref[...])
    for b in range(count):
        lo, hi = b * TILE, (b + 1) * TILE
        strip = dot_halves((high[:, lo:hi], low[:, lo:hi]), (high[:, lo:], low[:, lo:]))
        for c in range(b, count):
            blocks[b, c] = strip[:, (c - b) * TILE : (c - b + 1) * TILE]
    extra = [projected[:, b * TILE : (b + 1) * TILE] for b in range(count)]
    for r, c, paired in table:
        if paired:
            extra.append(jnp.sum(jnp.where(row == col, blocks[c, c], 0.0), axis=0, keepdims=True))
    for p, (r, c, paired) in enumerate(table):
        where = flipped(p ^ me)
        if paired:
            block = jnp.where(row <= col, blocks[r, r], blocks[c, c])
        else:
            block = blocks[r, c]
        foot = jnp.concatenate(extra + [extra[0]] * (8 - len(extra)), axis=0) if p == 0 else jnp.zeros((8, TILE), jnp.float32)
        for ref, low in ((keep_ref, 0), (send_ref, PIECES // 2)):

            @pl.when((where >= low) & (where < low + PIECES // 2))
            def _():
                ref[where - low, :TILE, :] = block
                ref[where - low, TILE:, :] = foot


def factor_tile(block, cols_ref, ahead_ref):
    count = TILE // GROUP
    sub = lax.broadcasted_iota(jnp.int32, (8, TILE), 0)
    lane = lax.broadcasted_iota(jnp.int32, (8, TILE), 1)
    left = [block[8 * q : 8 * q + 8, :] for q in range(count)]
    right = [jnp.where(lane == sub + 8 * q, 1.0, 0.0).astype(jnp.float32) for q in range(count)]
    cols = [full(left[0][:, k : k + 1]) for k in range(GROUP)]
    for p in range(count):
        base = GROUP * p
        corner = 64 * p
        for k in range(GROUP):
            cols_ref[corner + 8 * k : corner + 8 * k + 8, :] = cols[k]
        a = [
            [cols_ref[pl.ds(corner + 8 * k + m, 8, stride=0), :] if m >= k else None for k in range(GROUP)]
            for m in range(GROUP)
        ]
        if p + 1 < count:
            cols = [full(left[p + 1][:, base + 8 + k : base + 9 + k]) for k in range(GROUP)]
        low = [[None] * GROUP for _ in range(GROUP)]
        root = []
        for k in range(GROUP):
            root.append(lax.rsqrt(a[k][k]))
            inverse = root[k] * root[k]
            for m in range(k + 1, GROUP):
                for j in range(k + 1, m + 1):
                    a[m][j] = a[m][j] - (a[m][k] * a[j][k]) * inverse
        for k in range(GROUP):
            for m in range(k + 1, GROUP):
                low[m][k] = a[m][k] * root[k]
        upper = [full(left[p][k : k + 1, :]) for k in range(GROUP)]
        other = [full(right[p][k : k + 1, :]) for k in range(GROUP)]
        for k in range(GROUP):
            upper[k] = upper[k] * root[k]
            other[k] = other[k] * root[k]
            for m in range(k + 1, GROUP):
                upper[m] = upper[m] - low[m][k] * upper[k]
                other[m] = other[m] - low[m][k] * other[k]
        for q in range(p + 1, count):
            c = [full(left[q][:, base + k : base + k + 1]) for k in range(GROUP)]
            for k in range(GROUP):
                c[k] = c[k] * root[k]
                for m in range(k + 1, GROUP):
                    c[m] = c[m] - low[m][k] * c[k]
            if q == p + 1:
                for k in range(GROUP):
                    ahead_ref[corner + 8 * k : corner + 8 * k + 8, :] = c[k]
                for m in range(GROUP):
                    for k in range(GROUP):
                        cols[m] = cols[m] - c[k] * ahead_ref[pl.ds(corner + 8 * k + m, 8, stride=0), :]
            for k in range(GROUP):
                left[q] = left[q] - c[k] * upper[k]
                right[q] = right[q] - c[k] * other[k]
        new_left, new_right = upper[GROUP - 1], other[GROUP - 1]
        for k in range(GROUP - 1):
            new_left = jnp.where(sub == k, upper[k], new_left)
            new_right = jnp.where(sub == k, other[k], new_right)
        left[p] = jnp.where(lane >= sub + base, new_left, 0.0)
        right[p] = new_right
    return left, right


def factor_kernel(table, groups, me_ref, *refs):
    sources = refs[: len(groups)]
    feat_ref, misfit_ref, deriv_ref, params_ref, upper_ref, new_ref, resid_ref, stage, work, inv, rhs, cols_ref, ahead_ref = refs[len(groups) :]
    terms = work.shape[0]
    count = terms // TILE
    me = me_ref[0]
    for source, places in zip(sources, groups):
        for k, place in enumerate(places):
            stage[place ^ me] = source[k]
    row = lax.broadcasted_iota(jnp.int32, (TILE, TILE), 0)
    col = lax.broadcasted_iota(jnp.int32, (TILE, TILE), 1)
    damp = jnp.where(row == col, DAMPING, 0.0)
    extra = count
    for p, (r, c, paired) in enumerate(table):
        block = stage[p, :TILE, :]
        if paired:
            turned = block.T
            diag = stage[0, TILE + extra : TILE + extra + 1, :]
            extra += 1
            work[r * TILE : (r + 1) * TILE, r * TILE : (r + 1) * TILE] = jnp.where(row <= col, block, turned) + damp
            second = jnp.where(row == col, diag, jnp.where(row > col, block, turned))
            work[c * TILE : (c + 1) * TILE, c * TILE : (c + 1) * TILE] = second + damp
        else:
            work[r * TILE : (r + 1) * TILE, c * TILE : (c + 1) * TILE] = block
    for b in range(count):
        rhs[:, b * TILE : (b + 1) * TILE] = full(stage[0, TILE + b : TILE + b + 1, :])
    upper_ref[...] = jnp.zeros_like(upper_ref)

    def step(b, carry):
        off = pl.multiple_of(b * TILE, TILE)
        left, right = factor_tile(work[pl.ds(off, TILE), pl.ds(off, TILE)], cols_ref, ahead_ref)
        for q in range(TILE // GROUP):
            upper_ref[pl.ds(off + 8 * q, 8), pl.ds(off, TILE)] = left[q]
            inv[pl.ds(off + 8 * q, 8), :] = right[q]
        for bb in range(count):

            @pl.when(b == bb)
            def _():
                lo, hi = bb * TILE, (bb + 1) * TILE
                solved = dot_columns(rhs[:, lo:hi], inv[lo:hi, :])
                rhs[:, lo:hi] = solved
                if hi < terms:
                    panel = dot_plain(inv[lo:hi, :], work[lo:hi, hi:])
                    upper_ref[lo:hi, hi:] = panel
                    rhs[:, hi:] -= dot_plain(solved, panel)
                    for r in range(bb + 1, count):
                        s = (r - bb - 1) * TILE
                        work[r * TILE : (r + 1) * TILE, r * TILE :] -= dot_rows(panel[:, s : s + TILE], panel[:, s:])

        return carry

    lax.fori_loop(0, count, step, 0)
    for b in range(count - 1, -1, -1):
        lo, hi = b * TILE, (b + 1) * TILE
        rest = rhs[:, lo:hi]
        if hi < terms:
            rest = rest - dot_columns(rhs[:, hi:], upper_ref[lo:hi, hi:])
        rhs[:, lo:hi] = dot_plain(rest, inv[lo:hi, :])
    update = rhs[0:1, :]
    new_ref[...] = params_ref[...] + update
    gauges, doses = misfit_ref.shape
    lane = lax.broadcasted_iota(jnp.int32, (gauges, doses), 1)
    moved = jnp.zeros((gauges, doses), jnp.float32)
    for d in range(doses):
        along = jnp.sum(feat_ref[d * gauges : (d + 1) * gauges, :] * update, axis=1, keepdims=True)
        moved = jnp.where(lane == d, along, moved)
    resid_ref[...] = misfit_ref[...] - deriv_ref[...] * moved


def local(
    aerial_clips,
    basis_terms,
    holder,
    cache_slot,
    dose_index,
    dose_levels,
    threshold,
    measured,
    parameters,
):
    gauge_count = lax.axis_size("gauge")
    focus_count = lax.axis_size("focus")
    me = lax.axis_index("gauge")
    core = me & 1
    clips = aerial_clips[0]
    cached, pixels = clips.shape
    gauges = holder.shape[1]
    doses = dose_index.shape[2]
    terms = basis_terms.shape[1]
    half = pixels // 2
    step = half // CHUNKS
    gauge_bits = bits_of(gauge_count)
    offsets = list(range(0, gauge_count, 2))
    wide = gauge_bits[1:]

    notes = jnp.concatenate([holder[0], cache_slot[0], dose_index[0]], axis=1)
    theirs_notes = swap(notes, "gauge", 1)
    chunks = []
    for k in range(CHUNKS):
        if k == 1:
            clips, chunks[0][0] = lax.optimization_barrier((clips, chunks[0][0]))
        mine = lax.dynamic_slice(clips, (0, core * half + k * step), (cached, step))
        theirs = lax.dynamic_slice(clips, (0, (1 - core) * half + k * step), (cached, step))
        block = jnp.concatenate([mine, swap(theirs, "gauge", 1)], axis=0)
        order = wide if k % 2 == 0 else wide[::-1]
        if k > 1:
            before = chunks[k - 2]
            block, before[order[0]] = lax.optimization_barrier((block, before[order[0]]))
        pieces, have = {0: block}, [0]
        for bit in order:
            for o in list(have):
                pieces[o ^ bit] = swap(pieces[o], "gauge", bit)
                have.append(o ^ bit)
        chunks.append(pieces)

    def orders(own, values):
        relative = values[:, 0:2] ^ own
        place = relative * cached + values[:, 2:4]
        spots = jnp.arange(gauge_count * cached, dtype=jnp.int32)[None, :]
        select = jnp.where(place[:, 0:1] == spots, 0.5, 0.0) + jnp.where(place[:, 1:2] == spots, 0.5, 0.0)
        level = jnp.arange(dose_levels.shape[0], dtype=jnp.int32)
        chosen = (values[:, 4:, None] == level[None, None, :]).astype(jnp.float32)
        return STEEPNESS * jnp.sum(chosen * dose_levels[None, None, :], axis=2), select.astype(jnp.bfloat16)

    anchor = chunks[0][wide[0]]
    notes, theirs_notes, anchor = lax.optimization_barrier((notes, theirs_notes, anchor))
    chunks[0][wide[0]] = anchor
    mine_orders, their_orders = orders(me, notes), orders(me, theirs_notes)
    dose, select = [jnp.concatenate(both, axis=0) for both in zip(mine_orders, their_orders)]
    level = STEEPNESS * threshold
    totals = None
    for k in range(0, CHUNKS, TOGETHER):
        start = (core * half + k * step).astype(jnp.int32)[None]
        held = [chunk[o] for chunk in chunks[k : k + TOGETHER] for o in offsets]
        totals = resist_rows(start, level, dose, select, held, basis_terms, totals)
    mine_total, their_total = totals
    rows = gauges * doses
    other = swap(their_total, "gauge", 1)

    count = terms // TILE
    table = piece_table(count)
    scale = float(rows * gauge_count * focus_count) ** (-0.5)
    slot = (me % PIECES).astype(jnp.int32)[None]
    feat, misfit, deriv, kept, sent = pl.pallas_call(
        functools.partial(normal_kernel, scale, table),
        in_specs=[SMEM] + [VMEM] * 4,
        out_specs=(VMEM,) * 5,
        out_shape=(
            jax.ShapeDtypeStruct((rows, terms), jnp.float32),
            jax.ShapeDtypeStruct((gauges, doses), jnp.float32),
            jax.ShapeDtypeStruct((gauges, doses), jnp.float32),
            jax.ShapeDtypeStruct((PIECES // 2, PIECE_ROWS, TILE), jnp.float32),
            jax.ShapeDtypeStruct((PIECES // 2, PIECE_ROWS, TILE), jnp.float32),
        ),
        scratch_shapes=[pltpu.VMEM((rows, terms), jnp.float32)],
        compiler_params=pltpu.CompilerParams(vmem_limit_bytes=VMEM_BYTES),
        name="normal",
    )(slot, mine_total, other, measured[0], parameters[None, :])

    first, near, others = gauge_bits[0], gauge_bits[1:HALVINGS], gauge_bits[HALVINGS:]
    ways = [sum(bit for n, bit in enumerate(near) if (p >> (len(near) - 1 - n)) & 1) for p in range(PIECES // 2)]
    got = swap(sent, "gauge", first)
    parts = [kept[p : p + 1] + got[p : p + 1] for p in range(PIECES // 2)]
    terms_in = [parts[0]] + [swap(parts[p], "gauge", ways[p]) for p in range(1, PIECES // 2)]
    current = add_pairs(terms_in)
    current = exchange(current, "gauge", others)
    current = exchange(current, "focus", bits_of(focus_count))
    parts = [current] + [swap(current, "gauge", way) for way in ways[1:]]
    parts = parts + [swap(part, "gauge", first) for part in parts]
    order = list(range(PIECES))
    groups = [[flipped(k)] for k in order]

    upper, new_params, residual = pl.pallas_call(
        functools.partial(factor_kernel, table, groups),
        in_specs=[SMEM] + [VMEM] * (len(parts) + 4),
        out_specs=(VMEM, VMEM, VMEM),
        out_shape=(
            jax.ShapeDtypeStruct((terms, terms), jnp.float32),
            jax.ShapeDtypeStruct((1, terms), jnp.float32),
            jax.ShapeDtypeStruct((gauges, doses), jnp.float32),
        ),
        scratch_shapes=[
            pltpu.VMEM((PIECES, PIECE_ROWS, TILE), jnp.float32),
            pltpu.VMEM((terms, terms), jnp.float32),
            pltpu.VMEM((terms, TILE), jnp.float32),
            pltpu.VMEM((8, terms), jnp.float32),
            pltpu.VMEM((TILE * GROUP, TILE), jnp.float32),
            pltpu.VMEM((TILE * GROUP, TILE), jnp.float32),
        ],
        compiler_params=pltpu.CompilerParams(vmem_limit_bytes=VMEM_BYTES),
        name="factor",
    )(slot, *parts, feat, misfit, deriv, parameters[None, :])
    return upper, new_params[0], residual[None]


def solution(mesh):
    return jax.shard_map(
        local,
        mesh=mesh,
        in_specs=(
            P("focus", "gauge", None),
            P(),
            P("focus", "gauge", None),
            P("focus", "gauge", None),
            P("focus", "gauge", None),
            P(),
            P("focus"),
            P("focus", "gauge", None),
            P(),
        ),
        out_specs=(P(), P(), P("focus", "gauge", None)),
        check_vma=False,
    )
```
